256 devices in a mesh: dp: 32 (over z, x), rows: 8 (over y, core).
Axes of the slice: x: 4, y: 4, z: 8, core: 2. Of those that a mesh axis runs over, the one named last changes fastest.
Arguments:
- token_ids: int32 [256, 128], P(('dp', 'rows')), may hold values from 0 to 8191, as said below
- upstream: bfloat16 [256, 128, 5376], P(('dp', 'rows')), may hold values from -6 to 6
- saved_rows: bfloat16 [256, 128, 5376], P(('dp', 'rows')), may hold values from -4 to 4
- norm_gain: float32 [5376], replicated, may hold values from 0.5 to 1.5
- master: float32 [8192, 5376], P('rows', 'dp'), may hold values from -6 to 6
- moment_one: float32 [8192, 5376], P('rows', 'dp'), may hold values from -4 to 4
- moment_two: float32 [8192, 5376], P('rows', 'dp'), may hold values from 0.1 to 4
Outputs:
- master_new: float32 [8192, 5376], P('rows', 'dp')
- moment_one_new: float32 [8192, 5376], P('rows', 'dp')
- moment_two_new: float32 [8192, 5376], P('rows', 'dp')
- new_rows: bfloat16 [256, 128, 5376], P(('dp', 'rows'))
The draws below stay inside these ranges and needn't reach their ends.
Inputs may be any that keep to these rules, and one draw needn't show every extreme that they name: `token_ids`: rows v with v // 1024 = k belong to owner k. In each sequence, one owner receives exactly 32 of its tokens and every other owner at most 32.
All inputs are finite; a program needn't handle non-finite values.
Results may differ from the reference program's by a relative error of at most 0.007.
Values may be sent and summed in bfloat16 or wider, within the bound.
A program may use at most 64 MiB of HBM per device.

```python
import math
import jax
import jax.numpy as jnp
from jax import lax

D = 5376
TOK = 128
VROWS_DEV = 1024
SEQS = 256
VOCAB = 8192
N_ROWS = 8


def draw_token_ids(key, part):
    hot_count = TOK // 4
    keys = jax.random.split(jax.random.fold_in(key, 7), 5)
    hot_owner = jax.random.randint(keys[0], (SEQS, 1), 0, N_ROWS)
    position = jnp.arange(TOK, dtype=jnp.int32)[None, :]
    offset = jnp.where(position < hot_count, 0, 1 + (position - hot_count) % (N_ROWS - 1))
    owner = (hot_owner + offset) % N_ROWS
    scores = jax.random.randint(keys[1], (SEQS, TOK), 0, 65536) * TOK + position
    order = jnp.argsort(scores, axis=1, stable=True)
    owner = jnp.take_along_axis(owner, order, axis=1)
    first = jax.random.randint(keys[2], (SEQS, TOK), 0, VROWS_DEV)
    second = jax.random.randint(keys[3], (SEQS, TOK), 0, VROWS_DEV)
    skewed = first * second // VROWS_DEV
    shuffle = jax.random.permutation(keys[4], VROWS_DEV).astype(jnp.int32)
    local = jnp.take(shuffle, skewed, axis=0)
    return (owner * VROWS_DEV + local).astype(jnp.int32)


def steps_of(stream_key, extent, cuts, low, high):
    def one(dim, parts):
        draws = jax.random.uniform(jax.random.fold_in(jax.random.fold_in(stream_key, 6), dim), (parts,), jnp.float32, low / len(cuts), high / len(cuts))
        return jnp.repeat(jnp.exp(draws), extent[dim] // parts).reshape((-1,) + (1,) * (len(extent) - dim - 1))

    loudness = one(*cuts[0])
    for cut in cuts[1:]:
        loudness = loudness * one(*cut)
    return loudness


def gaussian(rng, shape, deviation, most, shards=(), kind=jnp.bfloat16):
    entries = jax.random.normal(rng, shape, jnp.float32) * deviation
    if len(shards) > 0:
        entries = steps_of(rng, shape, shards, -0.22, 0.18) * entries
    return jnp.clip(entries, min=-most, max=most).astype(kind)


def setup_inputs(seed: int = 0) -> dict:
    seeds = jax.random.split(jax.random.key(seed), 8)
    token_ids = draw_token_ids(jax.random.fold_in(seeds[7], 71), 0)
    upstream = gaussian(seeds[1], (SEQS, TOK, D), 1.0, 6.0, ((0, 256),))
    saved_rows = gaussian(seeds[2], (SEQS, TOK, D), 0.5, 4.0, ((0, 256),))
    norm_gain = jnp.clip(1.0 + 0.1 * jax.random.normal(seeds[3], (D,), jnp.float32), 0.5, 1.5)
    master = gaussian(seeds[4], (VOCAB, D), 1.0, 6.0, ((0, 8), (1, 32)), jnp.float32)
    moment_one = gaussian(seeds[5], (VOCAB, D), 0.5, 4.0, ((0, 8), (1, 32)), jnp.float32)
    moment_two = jnp.clip(jnp.exp(math.log(4.0) - 3.6888794 * jax.random.uniform(seeds[6], (VOCAB, D), jnp.float32) ** steps_of(seeds[6], (VOCAB, D), ((0, 8), (1, 32)), -0.2, 0.2)), 0.1, 4.0)
    return dict(token_ids=token_ids, upstream=upstream, saved_rows=saved_rows, norm_gain=norm_gain, master=master, moment_one=moment_one, moment_two=moment_two)


def norm_back(upstream_rows, saved, gain):
    values = saved.astype(jnp.float32)
    row_mean = lax.optimization_barrier(jnp.mean(values, axis=-1, keepdims=True))
    centered = values - row_mean
    variance = lax.optimization_barrier(jnp.mean(centered * centered, axis=-1, keepdims=True))
    inv_std = lax.rsqrt(variance + 1e-05)
    normed = centered * inv_std
    scaled = upstream_rows.astype(jnp.float32) * gain
    mean_scaled = lax.optimization_barrier(jnp.mean(scaled, axis=-1, keepdims=True))
    mean_cross = lax.optimization_barrier(jnp.mean(scaled * normed, axis=-1, keepdims=True))
    return (inv_std * (scaled - mean_scaled - normed * mean_cross)).astype(jnp.bfloat16)

def reference(token_ids, upstream, saved_rows, norm_gain, master, moment_one, moment_two):
    vocab_rows = master.shape[0]

    def seq_grad(running, sequence):
        seq_ids, seq_up, seq_saved = sequence
        row_input = norm_back(seq_up, seq_saved, norm_gain)
        added = jax.ops.segment_sum(row_input.astype(jnp.float32), seq_ids, num_segments=vocab_rows)
        return (running + added, None)
    start_grad = jnp.zeros(master.shape, jnp.float32)
    row_grad, _ = lax.scan(seq_grad, start_grad, (token_ids, upstream, saved_rows))
    moment_one_new = 0.9 * moment_one + 0.1 * row_grad
    moment_two_new = 0.999 * moment_two + 0.001 * row_grad * row_grad
    first_fix = 1.0 - 0.9 ** 10
    second_fix = 1.0 - 0.999 ** 10
    update = moment_one_new / first_fix / (jnp.sqrt(moment_two_new / second_fix) + 1e-08) + 0.1 * master
    master_new = master - 0.05 * update
    new_rows = jnp.take(master_new.astype(jnp.bfloat16), token_ids, axis=0)
    return (master_new, moment_one_new, moment_two_new, new_rows)
```

```python
import functools

import jax
import jax.numpy as jnp
from jax import lax
from jax.experimental import pallas as pl
from jax.experimental.pallas import tpu as pltpu
from jax.sharding import PartitionSpec as P

MESH = pl.DeviceIdType.MESH
BF = jnp.bfloat16
F32 = jnp.float32
LANES = 128
NZ, NX, NY, NC = 8, 4, 4, 2
NDP, NROWS = NZ * NX, NY * NC


def norm_kernel(slice_width, up_ref, saved_ref, gain_ref, y_ref, turned):
    tokens, width = up_ref.shape
    pieces = width // LANES

    def part(i):
        return pl.ds(pl.multiple_of(i * LANES, LANES), LANES)

    def scaled_of(i):
        return up_ref[:, part(i)].astype(F32) * gain_ref[:, part(i)]

    def first(i, carried):
        total, total_scaled = carried
        return total + saved_ref[:, part(i)].astype(F32), total_scaled + scaled_of(i)

    zero = jnp.zeros((tokens, LANES), F32)
    total, total_scaled = lax.fori_loop(0, pieces, first, (zero, zero), unroll=2)
    mean = jnp.sum(total, axis=1, keepdims=True) / width
    mean_scaled = jnp.sum(total_scaled, axis=1, keepdims=True) / width

    def second(i, carried):
        squares, cross = carried
        centered = saved_ref[:, part(i)].astype(F32) - mean
        return squares + centered * centered, cross + scaled_of(i) * centered

    squares, cross = lax.fori_loop(0, pieces, second, (zero, zero), unroll=2)
    variance = jnp.sum(squares, axis=1, keepdims=True) / width
    inv_std = lax.rsqrt(variance + 1e-05)
    mean_cross = jnp.sum(cross, axis=1, keepdims=True) / width * inv_std

    def third(i, _):
        normed = (saved_ref[:, part(i)].astype(F32) - mean) * inv_std
        out = inv_std * (scaled_of(i) - mean_scaled - normed * mean_cross)
        turned[part(i), :] = out.T
        return 0

    lax.fori_loop(0, pieces, third, 0, unroll=2)

    def fourth(j, _):
        rows = pl.ds(pl.multiple_of(j * slice_width, 8), slice_width)
        y_ref[j] = turned[rows, :].astype(BF)
        return 0

    lax.fori_loop(0, width // slice_width, fourth, 0)


def adam(grad, master, one, two):
    one_new = 0.9 * one + 0.1 * grad
    two_new = 0.999 * two + 0.001 * grad * grad
    first_fix = 1.0 - 0.9**10
    second_fix = 1.0 - 0.999**10
    update = one_new / first_fix / (jnp.sqrt(two_new / second_fix) + 1e-08) + 0.1 * master
    return master - 0.05 * update, one_new, two_new


GROUP = 8


def step_kernel(
    ids_ref, y_ref, m_hbm, m1_hbm, m2_hbm, grad_ref, new_ref,
    ids_all, arrived, total, pair_out, pair_in, ring_out, ring_in, table, outgoing, state,
    ids_send, ids_recv, go_send, go_recv, back_send, back_recv,
    pair_send, pair_recv, ring_send, ring_recv, tab_send, tab_recv, local_sem,
):
    d = lax.axis_index("dp")
    r = lax.axis_index("rows")
    z, x = d // NX, d % NX
    y, c = r // NC, r % NC
    owned = grad_ref.shape[1]

    def ahead(off):
        return ((z + off // NX) % NZ) * NX + (x + off % NX) % NX

    def behind(off):
        return ((z + NZ - off // NX) % NZ) * NX + (x + NX - off % NX) % NX

    def row_peer(dy, dc):
        return ((y + dy) % NY) * NC + (c + dc) % NC

    def copy(src, dst, send, recv, dp=None, rows=None):
        return pltpu.make_async_remote_copy(
            src_ref=src, dst_ref=dst, send_sem=send, recv_sem=recv,
            device_id={"dp": d if dp is None else dp, "rows": r if rows is None else rows},
            device_id_type=MESH,
        )

    barrier = pltpu.get_barrier_semaphore()

    def greet(off, _):
        pl.semaphore_signal(barrier, inc=1, device_id={"dp": ahead(off), "rows": r}, device_id_type=MESH)
        return 0

    lax.fori_loop(1, NDP, greet, 0)
    for dy in range(1, NY):
        pl.semaphore_signal(barrier, inc=1, device_id={"dp": d, "rows": row_peer(dy, 0)}, device_id_type=MESH)
    pl.semaphore_signal(barrier, inc=1, device_id={"dp": d, "rows": row_peer(0, 1)}, device_id_type=MESH)
    state_copies = [
        pltpu.make_async_copy(hbm, state.at[i], local_sem.at[i])
        for i, hbm in enumerate((m_hbm, m1_hbm, m2_hbm))
    ]
    for one in state_copies:
        one.start()
    pl.semaphore_wait(barrier, NDP - 1 + NY)

    def ids_copy(off):
        return copy(ids_ref, ids_all.at[off], ids_send.at[off], ids_recv.at[off], dp=ahead(off))

    def go_copy(off):
        return copy(y_ref.at[ahead(off)], arrived.at[off], go_send.at[off], go_recv.at[off], dp=ahead(off))

    def send_ids(off, _):
        ids_copy(off).start()
        return 0

    def send_go(off, _):
        go_copy(off).start()
        return 0

    lax.fori_loop(1, NDP, send_ids, 0)
    lax.fori_loop(1, NDP, send_go, 0)
    ids_all[0] = ids_ref[...]
    arrived[0] = y_ref[d]
    total[...] = jnp.zeros_like(total)

    def hot(group, base):
        rows = lax.broadcasted_iota(jnp.int32, (owned, LANES), 0) + base
        return jnp.concatenate(
            [(rows == ids_all[group * GROUP + k]).astype(F32).astype(BF) for k in range(GROUP)], axis=1
        )

    def go_group(group, _):
        def wait(k, _):
            off = group * GROUP + k

            @pl.when(off > 0)
            def _():
                ids_copy(off).wait_recv()
                go_copy(off).wait_recv()

            return 0

        lax.fori_loop(0, GROUP, wait, 0)
        block = jnp.concatenate([arrived[group * GROUP + k] for k in range(GROUP)], axis=1)

        def owner_step(k, _):
            total[k] += lax.dot_general(
                block, hot(group, k * owned), (((1,), (1,)), ((), ())), preferred_element_type=F32
            )
            return 0

        lax.fori_loop(0, NROWS, owner_step, 0)
        return 0

    lax.fori_loop(0, NDP // GROUP, go_group, 0)

    def pair_copy(dy):
        return copy(
            pair_out.at[dy], pair_in.at[dy], pair_send.at[dy], pair_recv.at[dy], rows=row_peer(0, 1)
        )

    for dy in (2, 1, 3, 0):
        pair_out[dy] = total[row_peer(dy, 1)].astype(BF)
        pair_copy(dy).start()

    def ring_copy(dy):
        return copy(
            ring_out.at[dy], ring_in.at[dy], ring_send.at[dy], ring_recv.at[dy], rows=row_peer(dy, 0)
        )

    for dy in (2, 1, 3):
        pair_copy(dy).wait_recv()
        ring_out[dy] = (total[row_peer(dy, 0)] + pair_in[dy].astype(F32)).astype(BF)
        ring_copy(dy).start()
    pair_copy(0).wait_recv()
    grad = total[row_peer(0, 0)] + pair_in[0].astype(F32)
    for dy in (1, 3, 2):
        ring_copy(dy).wait_recv()
        grad = grad + ring_in[dy].astype(F32)
    grad_ref[...] = grad
    for one in state_copies:
        one.wait()
    table[r] = adam(grad_ref[...], state[0], state[1], state[2])[0].astype(BF)

    def spread_copy(dy):
        return copy(table.at[r], table.at[r], tab_send.at[dy], tab_recv.at[dy], rows=row_peer(dy, 0))

    def spread_wait(dy):
        k = row_peer(NY - dy, 0)
        copy(table.at[k], table.at[k], tab_send.at[dy], tab_recv.at[dy], rows=row_peer(dy, 0)).wait_recv()

    def hand_copy(dy, dc):
        k = row_peer(NY - dy, dc)
        return copy(
            table.at[k], table.at[k], tab_send.at[NY + dy], tab_recv.at[NY + dy], rows=row_peer(0, 1)
        )

    for dy in (2, 1, 3):
        spread_copy(dy).start()
    hand_copy(0, 0).start()
    for dy in (1, 3, 2):
        spread_wait(dy)
        hand_copy(dy, 0).start()
    for dy in (0, 1, 3, 2):
        hand_copy(dy, 1).wait_recv()

    def back_copy(off):
        return copy(
            outgoing.at[off], new_ref.at[d], back_send.at[off], back_recv.at[off], dp=behind(off)
        )

    def back_wait(off):
        slot = new_ref.at[ahead(off)]
        copy(slot, slot, back_send.at[off], back_recv.at[off], dp=behind(off)).wait_recv()

    def back_group(group, _):
        def owner_step(k, picked):
            return picked + jnp.dot(table[k], hot(group, k * owned), preferred_element_type=F32)

        picked = lax.fori_loop(
            0, NROWS, owner_step, jnp.zeros((grad_ref.shape[0], GROUP * LANES), F32)
        ).astype(BF)
        for k in range(GROUP):
            outgoing[group * GROUP + k] = picked[:, k * LANES:(k + 1) * LANES]

        def send(k, _):
            off = group * GROUP + k

            @pl.when(off > 0)
            def _():
                back_copy(off).start()

            return 0

        lax.fori_loop(0, GROUP, send, 0)
        return 0

    lax.fori_loop(0, NDP // GROUP, back_group, 0)
    new_ref[d] = outgoing[0]

    def finish(off, _):
        ids_copy(off).wait_send()
        go_copy(off).wait_send()
        back_copy(off).wait_send()
        back_wait(off)
        return 0

    lax.fori_loop(1, NDP, finish, 0)
    for dy in range(NY):
        pair_copy(dy).wait_send()
        hand_copy(dy, 0).wait_send()
        if dy:
            ring_copy(dy).wait_send()
            spread_copy(dy).wait_send()


def per_device(token_ids, upstream, saved_rows, norm_gain, master, moment_one, moment_two):
    owned, width = master.shape
    tokens, features = upstream.shape[1:]
    vmem = pl.BlockSpec(memory_space=pltpu.VMEM)
    hbm = pl.BlockSpec(memory_space=pl.ANY)
    limit = 60 * 1024 * 1024
    y = pl.pallas_call(
        functools.partial(norm_kernel, width),
        out_shape=jax.ShapeDtypeStruct((NDP, width, tokens), BF),
        in_specs=[vmem] * 3,
        out_specs=vmem,
        scratch_shapes=[pltpu.VMEM((features, tokens), F32)],
        compiler_params=pltpu.CompilerParams(vmem_limit_bytes=limit),
    )(upstream[0], saved_rows[0], norm_gain[None])
    turned = (master.T, moment_one.T, moment_two.T)
    dma = pltpu.SemaphoreType.DMA
    grad, new = pl.pallas_call(
        step_kernel,
        out_shape=(
            jax.ShapeDtypeStruct((width, owned), F32),
            jax.ShapeDtypeStruct((NDP, width, tokens), BF),
        ),
        in_specs=[vmem, vmem, hbm, hbm, hbm],
        out_specs=(vmem, vmem),
        scratch_shapes=[
            pltpu.VMEM((NDP, 1, tokens), jnp.int32),
            pltpu.VMEM((NDP, width, tokens), BF),
            pltpu.VMEM((NROWS, width, owned), F32),
            pltpu.VMEM((NY, width, owned), BF),
            pltpu.VMEM((NY, width, owned), BF),
            pltpu.VMEM((NY, width, owned), BF),
            pltpu.VMEM((NY, width, owned), BF),
            pltpu.VMEM((NROWS, width, owned), BF),
            pltpu.VMEM((NDP, width, tokens), BF),
            pltpu.VMEM((3, width, owned), F32),
            dma((NDP,)), dma((NDP,)), dma((NDP,)), dma((NDP,)), dma((NDP,)), dma((NDP,)),
            dma((NY,)), dma((NY,)), dma((NY,)), dma((NY,)), dma((2 * NY,)), dma((2 * NY,)),
            dma((3,)),
        ],
        compiler_params=pltpu.CompilerParams(
            collective_id=0, has_side_effects=True, vmem_limit_bytes=limit
        ),
    )(token_ids, y, *turned)
    outs = [one.T for one in adam(grad, *turned)]
    new_rows = new.reshape(features, tokens).T[None]
    return (*outs, new_rows)


def solution(mesh):
    return jax.shard_map(
        per_device,
        mesh=mesh,
        in_specs=(
            P(("dp", "rows"), None),
            P(("dp", "rows"), None, None),
            P(("dp", "rows"), None, None),
            P(),
            P("rows", "dp"),
            P("rows", "dp"),
            P("rows", "dp"),
        ),
        out_specs=(
            P("rows", "dp"),
            P("rows", "dp"),
            P("rows", "dp"),
            P(("dp", "rows"), None, None),
        ),
        check_vma=False,
    )
```

```python
import functools

import jax
import jax.numpy as jnp
from jax import lax
from jax.experimental import pallas as pl
from jax.experimental.pallas import tpu as pltpu
from jax.sharding import PartitionSpec as P

MESH = pl.DeviceIdType.MESH
BF = jnp.bfloat16
F32 = jnp.float32
LANES = 128
NZ, NX, NY, NC = 8, 4, 4, 2
NDP, NROWS = NZ * NX, NY * NC
CHUNKS = 3
QUARTERS = 4
PER_Q = NDP // QUARTERS
SEATS = LANES // 4
LAG_RING, LAG_ADAM, LAG_HAND, LAG_BACK = 4, 6, 8, 9
TICKS = QUARTERS * (CHUNKS - 1) + LAG_BACK + QUARTERS
NT = (((1,), (1,)), ((), ()))


def norm_back(up_ref, saved_ref, gain_ref, turned):
    tokens, width = up_ref.shape
    pieces = width // LANES

    def part(i):
        return pl.ds(pl.multiple_of(i * LANES, LANES), LANES)

    def scaled_of(i):
        return up_ref[:, part(i)].astype(F32) * gain_ref[pl.ds(i, 1), :]

    def first(i, carried):
        total, total_scaled = carried
        return total + saved_ref[:, part(i)].astype(F32), total_scaled + scaled_of(i)

    zero = jnp.zeros((tokens, LANES), F32)
    total, total_scaled = lax.fori_loop(0, pieces, first, (zero, zero), unroll=2)
    mean = jnp.sum(total, axis=1, keepdims=True) / width
    mean_scaled = jnp.sum(total_scaled, axis=1, keepdims=True) / width

    def second(i, carried):
        squares, cross = carried
        centered = saved_ref[:, part(i)].astype(F32) - mean
        return squares + centered * centered, cross + scaled_of(i) * centered

    squares, cross = lax.fori_loop(0, pieces, second, (zero, zero), unroll=2)
    variance = jnp.sum(squares, axis=1, keepdims=True) / width
    inv_std = lax.rsqrt(variance + 1e-05)
    mean_cross = jnp.sum(cross, axis=1, keepdims=True) / width * inv_std

    def third(i, _):
        normed = (saved_ref[:, part(i)].astype(F32) - mean) * inv_std
        out = inv_std * (scaled_of(i) - mean_scaled - normed * mean_cross)
        turned[part(i), :] = out.T
        return 0

    lax.fori_loop(0, pieces, third, 0, unroll=2)


def adam(grad, master, one, two):
    one_new = 0.9 * one + 0.1 * grad
    two_new = 0.999 * two + 0.001 * grad * grad
    first_fix = 1.0 - 0.9**10
    second_fix = 1.0 - 0.999**10
    update = one_new / first_fix / (jnp.sqrt(two_new / second_fix) + 1e-08) + 0.1 * master
    return master - 0.05 * update, one_new, two_new


def seat_plan(ids_ref, owned, plan_ref):
    shape = (LANES, LANES)
    ids = jnp.broadcast_to(ids_ref[...], shape).astype(F32)
    across = ids.astype(jnp.int32)
    down = ids.T.astype(jnp.int32)
    owner_across, owner_down = across // owned, down // owned
    row = lax.broadcasted_iota(jnp.int32, shape, 0)
    lane = lax.broadcasted_iota(jnp.int32, shape, 1)
    earlier = (owner_across == owner_down) & (row < lane)
    rank = jnp.sum(earlier.astype(F32), axis=0, keepdims=True)
    rank_down = jnp.broadcast_to(rank, shape).T.astype(jnp.int32)
    plan_ref[pl.ds(NROWS, 1), :] = owner_across[:1] * LANES + rank.astype(jnp.int32)
    seated = rank_down == lane % SEATS
    local = (down - owner_down * owned + 1).astype(F32)
    for k in range(NROWS):
        here = jnp.where(seated & (owner_down == k), local, 0.0)
        plan_ref[pl.ds(k, 1), :] = jnp.sum(here, axis=0, keepdims=True).astype(jnp.int32) - 1


def hot(rows, wanted):
    return (lax.broadcasted_iota(jnp.int32, (rows, LANES), 0) == wanted).astype(F32).astype(BF)


def step_kernel(
    ids_ref, up_hbm, saved_hbm, gain_ref, m_hbm, m1_hbm, m2_hbm, grad_ref, new_ref,
    up_ref, saved_ref, turned, state, plan, plans, seats, y_ref, arrived, slots, total,
    pair_out, pair_in, ring_out, ring_in, table, outgoing,
    plan_send, plan_recv, go_send, go_recv, back_send, back_recv,
    pair_send, pair_recv, ring_send, ring_recv, tab_send, tab_recv, local_sem,
):
    d = lax.axis_index("dp")
    r = lax.axis_index("rows")
    z, x = d // NX, d % NX
    y, c = r // NC, r % NC
    height, owned = grad_ref.shape[1:]

    def ahead(off):
        return ((z + off // NX) % NZ) * NX + (x + off % NX) % NX

    def behind(off):
        return ((z + NZ - off // NX) % NZ) * NX + (x + NX - off % NX) % NX

    def row_peer(dy, dc):
        return ((y + dy) % NY) * NC + (c + dc) % NC

    def copy(src, dst, send, recv, dp=None, rows=None):
        return pltpu.make_async_remote_copy(
            src_ref=src, dst_ref=dst, send_sem=send, recv_sem=recv,
            device_id={"dp": d if dp is None else dp, "rows": r if rows is None else rows},
            device_id_type=MESH,
        )

    loads = [
        pltpu.make_async_copy(hbm, ref, local_sem.at[i])
        for i, (hbm, ref) in enumerate((
            (up_hbm, up_ref), (saved_hbm, saved_ref),
            (m_hbm, state.at[0]), (m1_hbm, state.at[1]), (m2_hbm, state.at[2]),
        ))
    ]
    for load in loads:
        load.start()
    barrier = pltpu.get_barrier_semaphore()

    def greet(off, _):
        pl.semaphore_signal(barrier, inc=1, device_id={"dp": ahead(off), "rows": r}, device_id_type=MESH)
        return 0

    lax.fori_loop(1, NDP, greet, 0)
    for dy in range(1, NY):
        pl.semaphore_signal(barrier, inc=1, device_id={"dp": d, "rows": row_peer(dy, 0)}, device_id_type=MESH)
    pl.semaphore_signal(barrier, inc=1, device_id={"dp": d, "rows": row_peer(0, 1)}, device_id_type=MESH)

    def clear(i, _):
        total[i] = jnp.zeros_like(total[i])
        return 0

    lax.fori_loop(0, CHUNKS * NROWS, clear, 0)
    seat_plan(ids_ref, owned, plan)
    plans[0] = plan[...]
    for load in loads:
        load.wait()
    norm_back(up_ref, saved_ref, gain_ref, turned)
    pl.semaphore_wait(barrier, NDP - 1 + NY)

    def plan_copy(off):
        return copy(plan, plans.at[off], plan_send, plan_recv, dp=ahead(off))

    def send_plan(off, _):
        plan_copy(off).start()
        return 0

    lax.fori_loop(1, NDP, send_plan, 0)

    def fill(chunk, j):
        block = j * CHUNKS + chunk
        y_ref[block] = turned[pl.ds(pl.multiple_of(block * height, 8), height), :].astype(BF)
        return block

    def send_go(chunk):
        def send(off, _):
            block = fill(chunk, ahead(off))
            copy(
                y_ref.at[block], arrived.at[chunk * NDP + off],
                go_send, go_recv.at[chunk * QUARTERS + off // PER_Q], dp=ahead(off),
            ).start()
            return 0

        lax.fori_loop(1, NDP, send, 0)
        arrived[chunk * NDP] = turned[
            pl.ds(pl.multiple_of((d * CHUNKS + chunk) * height, 8), height), :
        ].astype(BF)

    def wait_recv(ref, sem, dp=None, rows=None):
        copy(ref, ref, sem, sem, dp=dp, rows=rows).wait_recv()

    def wait_send(ref, sem, dp=None, rows=None):
        copy(ref, ref, sem, sem, dp=dp, rows=rows).wait_send()

    send_go(0)

    def wanted_slots(q, k):
        return jnp.concatenate(
            [hot(owned, seats[q * 2 + g, pl.ds(k, 1), :]) for g in range(2)], axis=1
        )

    def wanted_seats(q, g):
        first = q * PER_Q + g * 4
        return jnp.concatenate(
            [hot(owned, plans[first + s, pl.ds(NROWS, 1), :] + s * SEATS) for s in range(4)], axis=1
        )

    def pair_copy(chunk, dy):
        i = chunk * NY + dy
        return copy(
            pair_out.at[i], pair_in.at[i], pair_send.at[i], pair_recv.at[i], rows=row_peer(0, 1)
        )

    def ring_copy(chunk, dy):
        i = chunk * NY + dy
        return copy(
            ring_out.at[i], ring_in.at[i], ring_send.at[i], ring_recv.at[i], rows=row_peer(dy, 0)
        )

    def spread_copy(chunk, dy):
        ref = table.at[chunk * NROWS + r]
        i = chunk * NROWS + dy
        return copy(ref, ref, tab_send.at[i], tab_recv.at[i], rows=row_peer(dy, 0))

    def spread_wait(chunk, dy):
        ref = table.at[chunk * NROWS + row_peer(NY - dy, 0)]
        i = chunk * NROWS + dy
        copy(ref, ref, tab_send.at[i], tab_recv.at[i], rows=row_peer(dy, 0)).wait_recv()

    def hand_copy(chunk, dy, dc):
        ref = table.at[chunk * NROWS + row_peer(NY - dy, dc)]
        i = chunk * NROWS + NY + dy
        return copy(ref, ref, tab_send.at[i], tab_recv.at[i], rows=row_peer(0, 1))

    def go_part(chunk, q):
        sem = go_recv.at[chunk * QUARTERS + q]
        start = chunk * NDP + q * PER_Q

        @pl.when(q == 0)
        def _():
            wait_recv(arrived.at[pl.ds(chunk * NDP + 1, PER_Q - 1)], sem, dp=ahead(1))

        @pl.when(q > 0)
        def _():
            wait_recv(arrived.at[pl.ds(start, PER_Q)], sem, dp=ahead(1))

        for g in range(2):
            block = jnp.concatenate([arrived[start + g * 4 + s] for s in range(4)], axis=1)
            part = lax.dot_general(
                block, wanted_seats(q, g), NT, preferred_element_type=F32
            ).astype(BF)
            for k in range(NROWS):
                slots[k, :, g * LANES:(g + 1) * LANES] = part[:, k * LANES:(k + 1) * LANES]
        for dc in (1, 0):
            for dy in (2, 1, 3, 0):
                k = row_peer(dy, dc)
                summed = total[chunk * NROWS + k] + lax.dot_general(
                    slots[k], wanted_slots(q, k), NT, preferred_element_type=F32
                )
                total[chunk * NROWS + k] = summed
                if dc:

                    @pl.when(q == QUARTERS - 1)
                    def _():
                        pair_out[chunk * NY + dy] = total[chunk * NROWS + k].astype(BF)
                        pair_copy(chunk, dy).start()

    def ring_part(chunk):
        for dy in (2, 1, 3):
            i = chunk * NY + dy
            pair_copy(chunk, dy).wait_recv()
            own = total[chunk * NROWS + row_peer(dy, 0)]
            ring_out[i] = (own + pair_in[i].astype(F32)).astype(BF)
            ring_copy(chunk, dy).start()

    def adam_part(chunk):
        pair_copy(chunk, 0).wait_recv()
        grad = total[chunk * NROWS + r] + pair_in[chunk * NY].astype(F32)
        for dy in (1, 3, 2):
            ring_copy(chunk, dy).wait_recv()
            grad = grad + ring_in[chunk * NY + dy].astype(F32)
        grad_ref[chunk] = grad
        rows = pl.ds(pl.multiple_of(chunk * height, 8), height)
        fresh = adam(grad, state[0, rows, :], state[1, rows, :], state[2, rows, :])[0]
        table[chunk * NROWS + r] = fresh.astype(BF)
        for dy in (2, 1, 3):
            spread_copy(chunk, dy).start()
        hand_copy(chunk, 0, 0).start()

    def hand_part(chunk):
        for dy in (1, 3, 2):
            spread_wait(chunk, dy)
            hand_copy(chunk, dy, 0).start()

    def back_part(chunk, q):
        @pl.when(q == 0)
        def _():
            for dy in range(NY):
                hand_copy(chunk, dy, 1).wait_recv()

        picked = [
            jnp.dot(
                table[chunk * NROWS + k], wanted_slots(q, k), preferred_element_type=F32
            ).astype(BF)
            for k in range(NROWS)
        ]
        for g in range(2):
            block = jnp.concatenate([p[:, g * LANES:(g + 1) * LANES] for p in picked], axis=1)
            part = jnp.dot(block, wanted_seats(q, g), preferred_element_type=F32).astype(BF)
            first = chunk * NDP + q * PER_Q + g * 4
            for s in range(4):
                outgoing[first + s] = part[:, s * LANES:(s + 1) * LANES]

        def send(s, _):
            off = q * PER_Q + s

            @pl.when(off > 0)
            def _():
                copy(
                    outgoing.at[chunk * NDP + off], new_ref.at[d * CHUNKS + chunk],
                    back_send, back_recv, dp=behind(off),
                ).start()

            return 0

        lax.fori_loop(0, PER_Q, send, 0)

        @pl.when(q == 0)
        def _():
            new_ref[d * CHUNKS + chunk] = outgoing[chunk * NDP]

    def tick(t, _):
        @pl.when((t % QUARTERS == 0) & (t < QUARTERS * (CHUNKS - 1)))
        def _():
            send_go(t // QUARTERS + 1)

        @pl.when(t == 0)
        def _():
            wait_recv(plans.at[pl.ds(1, NDP - 1)], plan_recv, dp=ahead(1))
            lane = lax.broadcasted_iota(jnp.int32, (NROWS, LANES), 1)
            for g in range(NDP // 4):
                merged = plans[g * 4, :NROWS, :]
                for s in range(1, 4):
                    merged = jnp.where(lane >= s * SEATS, plans[g * 4 + s, :NROWS, :], merged)
                seats[g] = merged

        @pl.when(t < QUARTERS * CHUNKS)
        def _():
            go_part(t // QUARTERS, t % QUARTERS)

        for lag, work in ((LAG_RING, ring_part), (LAG_ADAM, adam_part), (LAG_HAND, hand_part)):

            @pl.when((t >= lag) & (t % QUARTERS == lag % QUARTERS) & (t < lag + QUARTERS * CHUNKS))
            def _():
                work((t - lag) // QUARTERS)

        @pl.when(t >= LAG_BACK)
        def _():
            back_part((t - LAG_BACK) // QUARTERS, (t - LAG_BACK) % QUARTERS)

        return 0

    lax.fori_loop(0, TICKS, tick, 0)

    sent = (NDP - 1) * CHUNKS
    wait_send(plans.at[pl.ds(0, NDP - 1)], plan_send, dp=ahead(1))
    wait_send(arrived.at[pl.ds(0, sent)], go_send, dp=ahead(1))
    wait_send(outgoing.at[pl.ds(0, sent)], back_send, dp=ahead(1))

    def finish(chunk, _):
        for dy in range(NY):
            pair_copy(chunk, dy).wait_send()
            hand_copy(chunk, dy, 0).wait_send()
            if dy:
                ring_copy(chunk, dy).wait_send()
                spread_copy(chunk, dy).wait_send()
        return 0

    lax.fori_loop(0, CHUNKS, finish, 0)
    wait_recv(new_ref.at[pl.ds(0, sent)], back_recv, dp=ahead(1))


def per_device(token_ids, upstream, saved_rows, norm_gain, master, moment_one, moment_two):
    owned, width = master.shape
    tokens, features = upstream.shape[1:]
    height = width // CHUNKS
    vmem = pl.BlockSpec(memory_space=pltpu.VMEM)
    hbm = pl.BlockSpec(memory_space=pl.ANY)
    turned = (master.T, moment_one.T, moment_two.T)
    dma = pltpu.SemaphoreType.DMA
    blocks = NDP * CHUNKS
    rows_bf = lambda n: pltpu.VMEM((n, height, owned), BF)
    tokens_bf = lambda n: pltpu.VMEM((n, height, tokens), BF)
    grad, new = pl.pallas_call(
        step_kernel,
        out_shape=(
            jax.ShapeDtypeStruct((CHUNKS, height, owned), F32),
            jax.ShapeDtypeStruct((blocks, height, tokens), BF),
        ),
        in_specs=[vmem, hbm, hbm, vmem, hbm, hbm, hbm],
        out_specs=(vmem, vmem),
        scratch_shapes=[
            pltpu.VMEM((tokens, features), BF),
            pltpu.VMEM((tokens, features), BF),
            pltpu.VMEM((features, tokens), F32),
            pltpu.VMEM((3, width, owned), F32),
            pltpu.VMEM((2 * NROWS, tokens), jnp.int32),
            pltpu.VMEM((NDP, 2 * NROWS, tokens), jnp.int32),
            pltpu.VMEM((NDP // 4, NROWS, LANES), jnp.int32),
            tokens_bf(blocks),
            tokens_bf(blocks),
            pltpu.VMEM((NROWS, height, 2 * LANES), BF),
            pltpu.VMEM((CHUNKS * NROWS, height, owned), F32),
            rows_bf(CHUNKS * NY), rows_bf(CHUNKS * NY), rows_bf(CHUNKS * NY), rows_bf(CHUNKS * NY),
            rows_bf(CHUNKS * NROWS),
            tokens_bf(blocks),
            dma, dma, dma, dma((CHUNKS * QUARTERS,)), dma, dma,
            dma((CHUNKS * NY,)), dma((CHUNKS * NY,)), dma((CHUNKS * NY,)), dma((CHUNKS * NY,)),
            dma((CHUNKS * NROWS,)), dma((CHUNKS * NROWS,)),
            dma((5,)),
        ],
        compiler_params=pltpu.CompilerParams(
            collective_id=0, has_side_effects=True, vmem_limit_bytes=60 * 1024 * 1024
        ),
    )(token_ids, upstream[0], saved_rows[0], norm_gain.reshape(-1, LANES), *turned)
    outs = [one.T for one in adam(grad.reshape(width, owned), *turned)]
    new_rows = new.reshape(features, tokens).T[None]
    return (*outs, new_rows)


def solution(mesh):
    return jax.shard_map(
        per_device,
        mesh=mesh,
        in_specs=(
            P(("dp", "rows"), None),
            P(("dp", "rows"), None, None),
            P(("dp", "rows"), None, None),
            P(),
            P("rows", "dp"),
            P("rows", "dp"),
            P("rows", "dp"),
        ),
        out_specs=(
            P("rows", "dp"),
            P("rows", "dp"),
            P("rows", "dp"),
            P(("dp", "rows"), None, None),
        ),
        check_vma=False,
    )
```

```python
import functools

import jax
import jax.numpy as jnp
from jax import lax
from jax.experimental import pallas as pl
from jax.experimental.pallas import tpu as pltpu
from jax.sharding import PartitionSpec as P

MESH = pl.DeviceIdType.MESH
BF = jnp.bfloat16
F32 = jnp.float32
LANES = 128
NZ, NX, NY, NC = 8, 4, 4, 2
NDP, NROWS = NZ * NX, NY * NC
CHUNKS = 3
QUARTERS = 4
PER_Q = NDP // QUARTERS
SEATS = LANES // 4
LAG_RING, LAG_ADAM, LAG_HAND, LAG_BACK = 4, 6, 8, 9
TICKS = QUARTERS * (CHUNKS - 1) + LAG_BACK + QUARTERS
GO_AT = 1


def norm_back(up_ref, saved_ref, gain_ref, turned):
    tokens, width = up_ref.shape
    pieces = width // LANES

    def part(i):
        return pl.ds(pl.multiple_of(i * LANES, LANES), LANES)

    def scaled_of(i):
        return up_ref[:, part(i)].astype(F32) * gain_ref[pl.ds(i, 1), :]

    def first(i, carried):
        total, total_scaled = carried
        return total + saved_ref[:, part(i)].astype(F32), total_scaled + scaled_of(i)

    zero = jnp.zeros((tokens, LANES), F32)
    total, total_scaled = lax.fori_loop(0, pieces, first, (zero, zero), unroll=2)
    mean = jnp.sum(total, axis=1, keepdims=True) / width
    mean_scaled = jnp.sum(total_scaled, axis=1, keepdims=True) / width

    def second(i, carried):
        squares, cross = carried
        centered = saved_ref[:, part(i)].astype(F32) - mean
        return squares + centered * centered, cross + scaled_of(i) * centered

    squares, cross = lax.fori_loop(0, pieces, second, (zero, zero), unroll=2)
    variance = jnp.sum(squares, axis=1, keepdims=True) / width
    inv_std = lax.rsqrt(variance + 1e-05)
    mean_cross = jnp.sum(cross, axis=1, keepdims=True) / width * inv_std

    def third(i, _):
        normed = (saved_ref[:, part(i)].astype(F32) - mean) * inv_std
        out = inv_std * (scaled_of(i) - mean_scaled - normed * mean_cross)
        turned[part(i), :] = out.T
        return 0

    lax.fori_loop(0, pieces, third, 0, unroll=2)


def adam(grad, master, one, two):
    one_new = 0.9 * one + 0.1 * grad
    two_new = 0.999 * two + 0.001 * grad * grad
    first_fix = 1.0 - 0.9**10
    second_fix = 1.0 - 0.999**10
    update = one_new / first_fix / (jnp.sqrt(two_new / second_fix) + 1e-08) + 0.1 * master
    return master - 0.05 * update, one_new, two_new


def seat_plan(ids_ref, owned, plan_ref):
    shape = (LANES, LANES)
    ids = jnp.broadcast_to(ids_ref[...], shape).astype(F32)
    across = ids.astype(jnp.int32)
    down = ids.T.astype(jnp.int32)
    owner_across, owner_down = across // owned, down // owned
    row = lax.broadcasted_iota(jnp.int32, shape, 0)
    lane = lax.broadcasted_iota(jnp.int32, shape, 1)
    earlier = (owner_across == owner_down) & (row < lane)
    rank = jnp.sum(earlier.astype(F32), axis=0, keepdims=True)
    rank_down = jnp.broadcast_to(rank, shape).T.astype(jnp.int32)
    plan_ref[pl.ds(NROWS, 1), :] = owner_across[:1] * LANES + rank.astype(jnp.int32)
    seated = rank_down == lane % SEATS
    local = (down - owner_down * owned + 1).astype(F32)
    for k in range(NROWS):
        here = jnp.where(seated & (owner_down == k), local, 0.0)
        plan_ref[pl.ds(k, 1), :] = jnp.sum(here, axis=0, keepdims=True).astype(jnp.int32) - 1


def hot(rows, wanted):
    return (lax.broadcasted_iota(jnp.int32, (rows, LANES), 0) == wanted).astype(F32).astype(BF)


def step_kernel(
    ids_ref, up_hbm, saved_hbm, gain_ref, m_hbm, m1_hbm, m2_hbm, grad_ref, new_ref,
    up_ref, saved_ref, turned, state, plan, plans, seats, y_ref, arrived, slots, total,
    pair_out, pair_in, ring_out, ring_in, table, outgoing, columns,
    plan_send, plan_recv, go_send, go_recv, back_send, back_recv,
    pair_send, pair_recv, ring_send, ring_recv, tab_send, tab_recv, local_sem,
):
    d = lax.axis_index("dp")
    r = lax.axis_index("rows")
    z, x = d // NX, d % NX
    y, c = r // NC, r % NC
    height, owned = grad_ref.shape[1:]

    def ahead(off):
        return ((z + off // NX) % NZ) * NX + (x + off % NX) % NX

    def behind(off):
        return ((z + NZ - off // NX) % NZ) * NX + (x + NX - off % NX) % NX

    def row_peer(dy, dc):
        return ((y + dy) % NY) * NC + (c + dc) % NC

    def copy(src, dst, send, recv, dp=None, rows=None):
        return pltpu.make_async_remote_copy(
            src_ref=src, dst_ref=dst, send_sem=send, recv_sem=recv,
            device_id={"dp": d if dp is None else dp, "rows": r if rows is None else rows},
            device_id_type=MESH,
        )

    loads = [
        pltpu.make_async_copy(hbm, ref, local_sem.at[i])
        for i, (hbm, ref) in enumerate((
            (up_hbm, up_ref), (saved_hbm, saved_ref),
            (m_hbm, state.at[0]), (m1_hbm, state.at[1]), (m2_hbm, state.at[2]),
        ))
    ]
    for load in loads:
        load.start()
    barrier = pltpu.get_barrier_semaphore()

    def greet(off, _):
        pl.semaphore_signal(barrier, inc=1, device_id={"dp": ahead(off), "rows": r}, device_id_type=MESH)
        return 0

    lax.fori_loop(1, NDP, greet, 0)
    for dy in range(1, NY):
        pl.semaphore_signal(barrier, inc=1, device_id={"dp": d, "rows": row_peer(dy, 0)}, device_id_type=MESH)
    pl.semaphore_signal(barrier, inc=1, device_id={"dp": d, "rows": row_peer(0, 1)}, device_id_type=MESH)

    def clear(i, _):
        total[i] = jnp.zeros_like(total[i])
        return 0

    lax.fori_loop(0, CHUNKS * NROWS, clear, 0)
    seat_plan(ids_ref, owned, plan)
    plans[0] = plan[...]
    pl.semaphore_wait(barrier, NDP - 1 + NY)

    def plan_copy(off):
        return copy(plan, plans.at[off], plan_send, plan_recv, dp=ahead(off))

    def send_plan(off, _):
        plan_copy(off).start()
        return 0

    lax.fori_loop(1, NDP, send_plan, 0)
    for load in loads:
        load.wait()
    norm_back(up_ref, saved_ref, gain_ref, turned)

    def fill(chunk, j):
        block = j * CHUNKS + chunk
        y_ref[block] = turned[pl.ds(pl.multiple_of(block * height, 8), height), :].astype(BF)
        return block

    def send_go(chunk):
        def send(off, _):
            block = fill(chunk, ahead(off))
            copy(
                y_ref.at[block], arrived.at[chunk * NDP + off],
                go_send, go_recv.at[chunk * QUARTERS + off // PER_Q], dp=ahead(off),
            ).start()
            return 0

        lax.fori_loop(1, NDP, send, 0)
        arrived[chunk * NDP] = turned[
            pl.ds(pl.multiple_of((d * CHUNKS + chunk) * height, 8), height), :
        ].astype(BF)

    def wait_recv(ref, sem, dp=None, rows=None):
        copy(ref, ref, sem, sem, dp=dp, rows=rows).wait_recv()

    def wait_send(ref, sem, dp=None, rows=None):
        copy(ref, ref, sem, sem, dp=dp, rows=rows).wait_send()

    send_go(0)

    def wanted_slots(q, k):
        return jnp.concatenate(
            [hot(owned, seats[q * 2 + g, pl.ds(k, 1), :]) for g in range(2)], axis=1
        )

    def wanted_seats(q, g):
        first = q * PER_Q + g * 4
        return jnp.concatenate(
            [hot(owned, plans[first + s, pl.ds(NROWS, 1), :] + s * SEATS) for s in range(4)], axis=1
        )

    def slot_columns(q, k):
        lane = lax.broadcasted_iota(jnp.int32, (LANES, owned), 1)
        return jnp.concatenate(
            [(lane == columns[q * 2 + g, :, k:k + 1]).astype(F32).astype(BF) for g in range(2)], axis=0
        )

    def seat_columns(q, g):
        lane = lax.broadcasted_iota(jnp.int32, (LANES, NROWS * LANES), 1)
        return jnp.concatenate(
            [
                (lane == columns[q * 2 + g, :, NROWS + s:NROWS + s + 1]).astype(F32).astype(BF)
                for s in range(4)
            ],
            axis=0,
        )

    def pair_copy(chunk, dy):
        i = chunk * NY + dy
        return copy(
            pair_out.at[i], pair_in.at[i], pair_send.at[i], pair_recv.at[i], rows=row_peer(0, 1)
        )

    def ring_copy(chunk, dy):
        i = chunk * NY + dy
        return copy(
            ring_out.at[i], ring_in.at[i], ring_send.at[i], ring_recv.at[i], rows=row_peer(dy, 0)
        )

    def spread_copy(chunk, dy):
        ref = table.at[chunk * NROWS + r]
        i = chunk * NROWS + dy
        return copy(ref, ref, tab_send.at[i], tab_recv.at[i], rows=row_peer(dy, 0))

    def spread_wait(chunk, dy):
        ref = table.at[chunk * NROWS + row_peer(NY - dy, 0)]
        i = chunk * NROWS + dy
        copy(ref, ref, tab_send.at[i], tab_recv.at[i], rows=row_peer(dy, 0)).wait_recv()

    def hand_copy(chunk, dy, dc):
        ref = table.at[chunk * NROWS + row_peer(NY - dy, dc)]
        i = chunk * NROWS + NY + dy
        return copy(ref, ref, tab_send.at[i], tab_recv.at[i], rows=row_peer(0, 1))

    def go_part(chunk, q):
        sem = go_recv.at[chunk * QUARTERS + q]
        start = chunk * NDP + q * PER_Q

        @pl.when(q == 0)
        def _():
            wait_recv(arrived.at[pl.ds(chunk * NDP + 1, PER_Q - 1)], sem, dp=ahead(1))

        @pl.when(q > 0)
        def _():
            wait_recv(arrived.at[pl.ds(start, PER_Q)], sem, dp=ahead(1))

        for g in range(2):
            block = jnp.concatenate([arrived[start + g * 4 + s] for s in range(4)], axis=1)
            part = jnp.dot(block, seat_columns(q, g), preferred_element_type=F32).astype(BF)
            for k in range(NROWS):
                slots[k, :, g * LANES:(g + 1) * LANES] = part[:, k * LANES:(k + 1) * LANES]
        for k in range(NROWS):
            total[chunk * NROWS + k] += jnp.dot(
                slots[k], slot_columns(q, k), preferred_element_type=F32
            )

        @pl.when(q == QUARTERS - 1)
        def _():
            for dy in (2, 1, 3, 0):
                pair_out[chunk * NY + dy] = total[chunk * NROWS + row_peer(dy, 1)].astype(BF)
                pair_copy(chunk, dy).start()

    def ring_part(chunk):
        for dy in (2, 1, 3):
            i = chunk * NY + dy
            pair_copy(chunk, dy).wait_recv()
            own = total[chunk * NROWS + row_peer(dy, 0)]
            ring_out[i] = (own + pair_in[i].astype(F32)).astype(BF)
            ring_copy(chunk, dy).start()

    def adam_part(chunk):
        pair_copy(chunk, 0).wait_recv()
        grad = total[chunk * NROWS + r] + pair_in[chunk * NY].astype(F32)
        for dy in (1, 3, 2):
            ring_copy(chunk, dy).wait_recv()
            grad = grad + ring_in[chunk * NY + dy].astype(F32)
        grad_ref[chunk] = grad
        rows = pl.ds(pl.multiple_of(chunk * height, 8), height)
        fresh = adam(grad, state[0, rows, :], state[1, rows, :], state[2, rows, :])[0]
        table[chunk * NROWS + r] = fresh.astype(BF)
        for dy in (2, 1, 3):
            spread_copy(chunk, dy).start()
        hand_copy(chunk, 0, 0).start()

    def hand_part(chunk):
        for dy in (1, 3, 2):
            spread_wait(chunk, dy)
            hand_copy(chunk, dy, 0).start()

    def back_part(chunk, q):
        @pl.when(q == 0)
        def _():
            for dy in range(NY):
                hand_copy(chunk, dy, 1).wait_recv()

        picked = [
            jnp.dot(
                table[chunk * NROWS + k], wanted_slots(q, k), preferred_element_type=F32
            ).astype(BF)
            for k in range(NROWS)
        ]
        for g in range(2):
            block = jnp.concatenate([p[:, g * LANES:(g + 1) * LANES] for p in picked], axis=1)
            part = jnp.dot(block, wanted_seats(q, g), preferred_element_type=F32).astype(BF)
            first = chunk * NDP + q * PER_Q + g * 4
            for s in range(4):
                outgoing[first + s] = part[:, s * LANES:(s + 1) * LANES]

        def send(s, _):
            off = q * PER_Q + s

            @pl.when(off > 0)
            def _():
                copy(
                    outgoing.at[chunk * NDP + off], new_ref.at[d * CHUNKS + chunk],
                    back_send, back_recv, dp=behind(off),
                ).start()

            return 0

        lax.fori_loop(0, PER_Q, send, 0)

        @pl.when(q == 0)
        def _():
            new_ref[d * CHUNKS + chunk] = outgoing[chunk * NDP]

    def tick(t, _):
        @pl.when((t % QUARTERS == GO_AT) & (t < QUARTERS * (CHUNKS - 1)))
        def _():
            send_go(t // QUARTERS + 1)

        @pl.when(t == 0)
        def _():
            wait_recv(plans.at[pl.ds(1, NDP - 1)], plan_recv, dp=ahead(1))
            lane = lax.broadcasted_iota(jnp.int32, (NROWS, LANES), 1)
            for g in range(NDP // 4):
                merged = plans[g * 4, :NROWS, :]
                for s in range(1, 4):
                    merged = jnp.where(lane >= s * SEATS, plans[g * 4 + s, :NROWS, :], merged)
                seats[g] = merged
                goals = [plans[g * 4 + s, pl.ds(NROWS, 1), :] + s * SEATS for s in range(4)]
                both = jnp.concatenate([merged] + goals + goals, axis=0).astype(F32)
                columns[g] = both.T.astype(jnp.int32)

        @pl.when(t < QUARTERS * CHUNKS)
        def _():
            go_part(t // QUARTERS, t % QUARTERS)

        for lag, work in ((LAG_RING, ring_part), (LAG_ADAM, adam_part), (LAG_HAND, hand_part)):

            @pl.when((t >= lag) & (t % QUARTERS == lag % QUARTERS) & (t < lag + QUARTERS * CHUNKS))
            def _():
                work((t - lag) // QUARTERS)

        @pl.when(t >= LAG_BACK)
        def _():
            back_part((t - LAG_BACK) // QUARTERS, (t - LAG_BACK) % QUARTERS)

        return 0

    lax.fori_loop(0, TICKS, tick, 0)

    sent = (NDP - 1) * CHUNKS
    wait_send(plans.at[pl.ds(0, NDP - 1)], plan_send, dp=ahead(1))
    wait_send(arrived.at[pl.ds(0, sent)], go_send, dp=ahead(1))
    wait_send(outgoing.at[pl.ds(0, sent)], back_send, dp=ahead(1))

    def finish(chunk, _):
        for dy in range(NY):
            pair_copy(chunk, dy).wait_send()
            hand_copy(chunk, dy, 0).wait_send()
            if dy:
                ring_copy(chunk, dy).wait_send()
                spread_copy(chunk, dy).wait_send()
        return 0

    lax.fori_loop(0, CHUNKS, finish, 0)
    wait_recv(new_ref.at[pl.ds(0, sent)], back_recv, dp=ahead(1))


def per_device(token_ids, upstream, saved_rows, norm_gain, master, moment_one, moment_two):
    owned, width = master.shape
    tokens, features = upstream.shape[1:]
    height = width // CHUNKS
    vmem = pl.BlockSpec(memory_space=pltpu.VMEM)
    hbm = pl.BlockSpec(memory_space=pl.ANY)
    turned = (master.T, moment_one.T, moment_two.T)
    dma = pltpu.SemaphoreType.DMA
    blocks = NDP * CHUNKS
    rows_bf = lambda n: pltpu.VMEM((n, height, owned), BF)
    tokens_bf = lambda n: pltpu.VMEM((n, height, tokens), BF)
    grad, new = pl.pallas_call(
        step_kernel,
        out_shape=(
            jax.ShapeDtypeStruct((CHUNKS, height, owned), F32),
            jax.ShapeDtypeStruct((blocks, height, tokens), BF),
        ),
        in_specs=[vmem, hbm, hbm, vmem, hbm, hbm, hbm],
        out_specs=(vmem, vmem),
        scratch_shapes=[
            pltpu.VMEM((tokens, features), BF),
            pltpu.VMEM((tokens, features), BF),
            pltpu.VMEM((features, tokens), F32),
            pltpu.VMEM((3, width, owned), F32),
            pltpu.VMEM((2 * NROWS, tokens), jnp.int32),
            pltpu.VMEM((NDP, 2 * NROWS, tokens), jnp.int32),
            pltpu.VMEM((NDP // 4, NROWS, LANES), jnp.int32),
            tokens_bf(blocks),
            tokens_bf(blocks),
            pltpu.VMEM((NROWS, height, 2 * LANES), BF),
            pltpu.VMEM((CHUNKS * NROWS, height, owned), F32),
            rows_bf(CHUNKS * NY), rows_bf(CHUNKS * NY), rows_bf(CHUNKS * NY), rows_bf(CHUNKS * NY),
            rows_bf(CHUNKS * NROWS),
            tokens_bf(blocks),
            pltpu.VMEM((NDP // 4, LANES, 2 * NROWS), jnp.int32),
            dma, dma, dma, dma((CHUNKS * QUARTERS,)), dma, dma,
            dma((CHUNKS * NY,)), dma((CHUNKS * NY,)), dma((CHUNKS * NY,)), dma((CHUNKS * NY,)),
            dma((CHUNKS * NROWS,)), dma((CHUNKS * NROWS,)),
            dma((5,)),
        ],
        compiler_params=pltpu.CompilerParams(
            collective_id=0, has_side_effects=True, vmem_limit_bytes=60 * 1024 * 1024
        ),
    )(token_ids, upstream[0], saved_rows[0], norm_gain.reshape(-1, LANES), *turned)
    outs = [one.T for one in adam(grad.reshape(width, owned), *turned)]
    new_rows = new.reshape(features, tokens).T[None]
    return (*outs, new_rows)


def solution(mesh):
    return jax.shard_map(
        per_device,
        mesh=mesh,
        in_specs=(
            P(("dp", "rows"), None),
            P(("dp", "rows"), None, None),
            P(("dp", "rows"), None, None),
            P(),
            P("rows", "dp"),
            P("rows", "dp"),
            P("rows", "dp"),
        ),
        out_specs=(
            P("rows", "dp"),
            P("rows", "dp"),
            P("rows", "dp"),
            P(("dp", "rows"), None, None),
        ),
        check_vma=False,
    )
```
